512 devices in a mesh: layer: 4 (over x), expert: 128 (over y, z, core).
Axes of the slice: x: 4, y: 4, z: 16, core: 2. Of those that a mesh axis runs over, the one named last changes fastest.
Arguments:
- grad_hidden: bfloat16 [131072, 384], P(('layer', 'expert')), parts along dimension 0, may hold values from -6 to 6
- grad_out: bfloat16 [131072, 1024], P(('layer', 'expert')), parts along dimension 0, may hold values from -0.41992188 to 0.41992188
- grad_route: int32 [131072, 1], P(('layer', 'expert')), parts along dimension 0, may hold values from 0 to 127; in each aligned block of 256 rows (0 to 255, 256 to 511, ...) at most 4 rows name the same one
- live_rows: int32 [512], P(('layer', 'expert')), parts along dimension 0, may hold values from 1 to 256, 24576 in all
- w_down: bfloat16 [512, 384, 1024], P(('layer', 'expert')), parts along dimension 0, may hold values from -0.3125 to 0.3125
- w_moment: bfloat16 [512, 384, 1024], P(('layer', 'expert')), parts along dimension 0, may hold values from -6 to 6
- perm: int32 [512], P('layer'), parts along dimension 0, may hold values from 0 to 127, each once
- fwd_hidden: bfloat16 [131072, 384], P(('layer', 'expert')), parts along dimension 0, may hold values from -6 to 6
- fwd_route: int32 [131072, 1], P(('layer', 'expert')), parts along dimension 0, may hold values from 0 to 127; in each aligned block of 256 rows (0 to 255, 256 to 511, ...) at most 4 rows name the same one
- fwd_gate: float32 [131072], P(('layer', 'expert')), parts along dimension 0, may hold values from 0.25 to 1
Outputs:
- placed_weight: bfloat16 [512, 384, 1024], P(('layer', 'expert')), parts along dimension 0
- placed_moment: bfloat16 [512, 384, 1024], P(('layer', 'expert')), parts along dimension 0
- fwd_out: bfloat16 [131072, 1024], P(('layer', 'expert')), parts along dimension 0
The draws below stay inside these ranges and needn't reach their ends.
There are 4 independent parts, one for each index of `layer`. The reference program is written for one: setup_inputs(seed, part) draws one part's arguments, and reference() takes and returns one part's arrays. A program takes and returns all parts, laid end to end along the dimension named above; each array names one. Nothing has to cross between parts.
Inputs may be any that keep to these rules, and one draw needn't show every extreme that they name: `grad_route`: among the 256 rows of one device no expert is named more than 4 times, and in some device's rows some expert is named exactly 4 times. `fwd_route`: among the 256 rows of one device no expert is named more than 4 times, and in some device's rows some expert is named exactly 4 times. `live_rows`: within each layer the counts sum to three quarters of 32768, and some device has all 256 rows live. `perm`: each device number appears once.
All inputs are finite; a program needn't handle non-finite values.
Results may differ from the reference program's by a relative error of at most 0.0065.
Values may be sent and summed in bfloat16 or wider, within the bound.
A program may use at most 64 MiB of HBM per device.

```python
import math
import jax
import jax.numpy as jnp
import numpy as np
from jax import lax

FF = 384
D = 1024
GRAD_DEV = 256
FWD_DEV = 256
EXPERTS = 128
CAP = 4
FCAP = 4
GRAD_ROWS = 32768
FWD_ROWS = 32768


def levels(stream_key, extent, cuts, least, high):
    level = 1.0
    for axis_at, blocks in cuts:
        steps = jax.random.uniform(jax.random.fold_in(jax.random.fold_in(stream_key, 6), axis_at), (blocks,), jnp.float32, least / len(cuts), high / len(cuts))
        level = level * jnp.repeat(jnp.exp(steps), extent[axis_at] // blocks).reshape((-1,) + (1,) * (len(extent) - 1 - axis_at))
    return level


def profile(amount, total, reach, lean):
    loads = [(1 << 20) // math.isqrt(grade ** lean) + 1 for grade in range(2, amount + 1)]
    spare, counts = total - reach - (amount - 1), [1] * (amount - 1)
    while spare > 0:
        candidates = [i for i in range(amount - 1) if counts[i] < reach]
        whole, remaining = sum([loads[i] for i in candidates]), spare
        for i in candidates:
            addition = min(reach - counts[i], max(1, remaining * loads[i] // whole), spare)
            counts[i] = counts[i] + addition
            spare = spare - addition
    return np.array([reach] + counts)


def uneven_parts(key, amount, total, most, slope):
    if amount == 2:
        one = jax.random.randint(key, (), max(1, total - most), min(most, total - 1) + 1)
        return jnp.stack([one, total - one])
    lengths = jnp.asarray(profile(amount, total, most, slope), jnp.int32)
    twos = (amount - 1) // 2
    source_of, sink = lengths[1:1 + 2 * twos:2], lengths[2:2 + 2 * twos:2]
    margin = jnp.minimum(source_of - 1, most - sink)
    moved = jax.random.randint(jax.random.fold_in(key, 1), (twos,), 0, 1 << 20) % (margin + 1)
    lengths = lengths.at[1:1 + 2 * twos:2].set(source_of - moved).at[2:2 + 2 * twos:2].set(sink + moved)
    return lengths[jax.random.permutation(jax.random.fold_in(key, 2), amount)]


def routed_block(stream_key, own, number, rows, amount, top, most, skew):
    ranking = jax.random.permutation(stream_key, amount)
    crowded, usual = load_shares(amount, rows * top, most, skew, True), load_shares(amount, rows * top, most, skew, False)
    places = jnp.arange(amount)

    def named(sizes, turn):
        used = int((sizes > 0).sum())
        fixed = max(1, used // 4)
        moved = fixed + (places - fixed + turn * (used - fixed)) % max(1, amount - fixed)
        return jnp.zeros((amount,), jnp.int32).at[ranking[jnp.where(places < fixed, places, moved)]].set(jnp.asarray(sizes, jnp.int32))

    sizes = jnp.where(number % 4 == 0, named(crowded, number // 4), named(usual, number - number // 4 - 1))
    mixed = jax.random.permutation(jax.random.fold_in(own, 3), amount)
    giver, receiver = mixed[0:amount // 2 * 2:2], mixed[1:amount // 2 * 2:2]
    margin = jnp.minimum(sizes[giver] - 1, most - sizes[receiver]) // 2
    margin = jnp.where((giver == ranking[0]) | (receiver == ranking[0]) | (sizes[receiver] == 0), 0, jnp.maximum(margin, 0))
    moved = jax.random.randint(jax.random.fold_in(own, 4), (amount // 2,), 0, 1 << 20) % (margin + 1)
    sizes = sizes.at[giver].add(-moved).at[receiver].add(moved)
    items = jnp.searchsorted(jnp.cumsum(sizes), jnp.arange(rows * top), side="right").astype(jnp.int32)
    listing = items.reshape(top, rows).T
    listing = listing[jax.random.permutation(jax.random.fold_in(own, 1), rows)]
    turn = jax.random.randint(jax.random.fold_in(own, 2), (rows, 1), 0, top)
    return jnp.take_along_axis(listing, (jnp.arange(top)[None, :] + turn) % top, axis=1)


def load_shares(number_of, total, reach, lean, full):
    weights = [(1 << 20) // math.isqrt(grade ** lean) + 1 for grade in range(1, number_of + 1)]
    largest = reach if full else min(reach, max(-(-total // number_of), total * weights[0] // sum(weights)))
    least = 1 if total - largest >= number_of - 1 else 0
    counts, rest = [largest] + [least] * (number_of - 1), total - largest - least * (number_of - 1)
    while rest > 0:
        free = [i for i in range(1, number_of) if counts[i] < largest] or [i for i in range(1, number_of) if counts[i] < reach]
        whole, budget = sum([weights[i] for i in free]), rest
        for i in free:
            addition = min(reach - counts[i], max(1, budget * weights[i] // whole), rest)
            counts[i] = counts[i] + addition
            rest = rest - addition
    return np.array(counts)


def noise(key, dims, deviation, limit, shards=(), held_as=jnp.bfloat16):
    drawn = jax.random.normal(key, dims, jnp.float32) * deviation
    if len(shards) > 0:
        drawn = levels(key, dims, shards, -0.22, 0.18) * drawn
    return jnp.clip(drawn, min=-limit, max=limit).astype(held_as)


def setup_inputs(seed: int = 0, part: int = 0) -> dict:
    streams_of = jax.random.split(jax.random.key(seed), 11)
    part_keys = jax.random.split(jax.random.fold_in(streams_of[10], part), 11)
    grad_hidden = noise(part_keys[0], (GRAD_ROWS, FF), 1.0, 6.0, ((0, 128),))
    grad_out = noise(part_keys[1], (GRAD_ROWS, D), 0.07, 0.41992188, ((0, 128),))
    grad_route_keys = jax.random.split(jax.random.fold_in(part_keys[2], 1), GRAD_ROWS // GRAD_DEV)
    grad_route_turns = jax.random.permutation(jax.random.fold_in(part_keys[2], 3), GRAD_ROWS // GRAD_DEV)
    grad_route = jax.vmap(lambda own, number: routed_block(jax.random.fold_in(part_keys[2], 2), own, number, GRAD_DEV, EXPERTS, 1, CAP, 2))(grad_route_keys, grad_route_turns).reshape((GRAD_ROWS, 1))
    live_rows = uneven_parts(part_keys[3], EXPERTS, 3 * GRAD_DEV * EXPERTS // 4, GRAD_DEV, 2).astype(jnp.int32)
    w_down = noise(part_keys[4], (EXPERTS, FF, D), FF ** -0.5, 0.3125, ((0, 128),))
    w_moment = noise(part_keys[5], (EXPERTS, FF, D), 1.0, 6.0, ((0, 128),))
    perm = jax.random.permutation(part_keys[6], EXPERTS).astype(jnp.int32)
    fwd_hidden = noise(part_keys[7], (FWD_ROWS, FF), 1.0, 6.0, ((0, 128),))
    fwd_route_keys = jax.random.split(jax.random.fold_in(part_keys[8], 1), FWD_ROWS // FWD_DEV)
    fwd_route_turns = jax.random.permutation(jax.random.fold_in(part_keys[8], 3), FWD_ROWS // FWD_DEV)
    fwd_route = jax.vmap(lambda own, number: routed_block(jax.random.fold_in(part_keys[8], 2), own, number, FWD_DEV, EXPERTS, 1, FCAP, 2))(fwd_route_keys, fwd_route_turns).reshape((FWD_ROWS, 1))
    fwd_gate = jnp.clip(0.25 + 0.75 * jax.random.uniform(part_keys[9], (FWD_ROWS,), jnp.float32) ** levels(part_keys[9], (FWD_ROWS,), ((0, 128),), -0.2, 0.2), 0.25, 1.0)
    return dict(grad_hidden=grad_hidden, grad_out=grad_out, grad_route=grad_route, live_rows=live_rows, w_down=w_down, w_moment=w_moment, perm=perm, fwd_hidden=fwd_hidden, fwd_route=fwd_route, fwd_gate=fwd_gate)


linear_term = 3.4445
cubic_term = -4.775
quintic_term = 2.0315
moment_decay = 0.9
step_scale = 0.25
norm_floor = 1e-07

def build_table(route_ids, is_live, width):
    total_rows = route_ids.shape[0]
    columns = jnp.arange(EXPERTS, dtype=jnp.int32)
    onehot = ((route_ids[:, None] == columns[None, :]) & is_live[:, None]).astype(jnp.int32)
    ranked = lax.optimization_barrier(jnp.sum(jnp.cumsum(onehot, axis=0) * onehot, axis=1)) - 1
    target = jnp.where(is_live, route_ids, EXPERTS).astype(jnp.int32)
    ranked = jnp.where(is_live, ranked, 0).astype(jnp.int32)
    table = jnp.full((EXPERTS, width), total_rows, dtype=jnp.int32)
    return table.at[target, ranked].set(jnp.arange(total_rows, dtype=jnp.int32), mode='drop')

def orthogonalize(moment):
    moment_f = moment.astype(jnp.float32)
    frobenius = jnp.sqrt(jnp.sum(moment_f * moment_f))
    current = (moment_f / (frobenius + norm_floor)).astype(jnp.bfloat16)
    for sweep_index in range(2):
        gramian = lax.dot_general(current, current, (((1,), (1,)), ((), ())), preferred_element_type=jnp.float32).astype(jnp.bfloat16)
        squared = jnp.dot(gramian, gramian, preferred_element_type=jnp.float32)
        poly = (cubic_term * gramian.astype(jnp.float32) + quintic_term * squared).astype(jnp.bfloat16)
        current = (linear_term * current.astype(jnp.float32) + jnp.dot(poly, current, preferred_element_type=jnp.float32)).astype(jnp.bfloat16)
    return current

def reference(grad_hidden, grad_out, grad_route, live_rows, w_down, w_moment, perm, fwd_hidden, fwd_route, fwd_gate):
    is_live = (jnp.arange(GRAD_DEV, dtype=jnp.int32)[None, :] < live_rows[:, None]).reshape(-1)
    table = build_table(grad_route[:, 0], is_live, EXPERTS * CAP)
    hidden_pad = jnp.concatenate([grad_hidden, jnp.zeros((1, FF), jnp.bfloat16)], axis=0)
    out_pad = jnp.concatenate([grad_out, jnp.zeros((1, D), jnp.bfloat16)], axis=0)

    def update_one(packed):
        row_ids, weight, moment = packed
        grad = jnp.dot(hidden_pad[row_ids].T, out_pad[row_ids], preferred_element_type=jnp.float32)
        moment_new = (moment_decay * moment.astype(jnp.float32) + grad).astype(jnp.bfloat16)
        ortho = orthogonalize(moment_new)
        weight_new = (weight.astype(jnp.float32) - step_scale * ortho.astype(jnp.float32)).astype(jnp.bfloat16)
        return (weight_new, moment_new)
    weight_new, moment_new = lax.map(update_one, (table, w_down, w_moment))
    placed_weight = jnp.zeros_like(weight_new).at[perm].set(weight_new)
    placed_moment = jnp.zeros_like(moment_new).at[perm].set(moment_new)
    total_fwd = fwd_hidden.shape[0]
    fwd_table = build_table(fwd_route[:, 0], jnp.ones((total_fwd,), dtype=bool), EXPERTS * FCAP)
    fwd_pad = jnp.concatenate([fwd_hidden, jnp.zeros((1, FF), jnp.bfloat16)], axis=0)

    def forward_one(packed):
        row_ids, weight = packed
        return jnp.dot(fwd_pad[row_ids], weight, preferred_element_type=jnp.float32).astype(jnp.bfloat16)
    expert_out = lax.map(forward_one, (fwd_table, weight_new))
    gathered = jnp.zeros((total_fwd + 1, D), jnp.bfloat16).at[fwd_table.reshape(-1)].set(expert_out.reshape(-1, D))[:total_fwd]
    fwd_out = (gathered.astype(jnp.float32) * fwd_gate[:, None]).astype(jnp.bfloat16)
    return (placed_weight, placed_moment, fwd_out)
```

```python
import jax
import jax.numpy as jnp
from jax import lax
from jax.experimental import pallas as pl
from jax.experimental.pallas import tpu as pltpu
from jax.sharding import PartitionSpec as P

linear_term = 3.4445
cubic_term = -4.775
quintic_term = 2.0315
moment_decay = 0.9
step_scale = 0.25
norm_floor = 1e-07

Y, Z = 4, 16
CHIPS = Y * Z
EXPERTS = 2 * CHIPS
CAP = 4
ROWS, FF, D = 256, 384, 1024
WIDE = FF + D
PR, PC = 48, 128
PCOLS = D // PC

f32, bf16, i32 = jnp.float32, jnp.bfloat16, jnp.int32


def dot(a, b, dims=(((1,), (0,)), ((), ()))):
    return lax.dot_general(a, b, dims, preferred_element_type=f32)


def piece(ref, p):
    return ref.at[
        pl.ds(pl.multiple_of((p // PCOLS) * PR, 16), PR),
        pl.ds(pl.multiple_of((p % PCOLS) * PC, 128), PC),
    ]


def slots_row(route_row, live):
    experts = lax.broadcasted_iota(i32, (EXPERTS, ROWS), 0)
    hit = experts == route_row
    if live is not None:
        hit = hit & (lax.broadcasted_iota(i32, (EXPERTS, ROWS), 1) < live)
    onehot = jnp.where(hit, 1.0, 0.0)
    r = lax.broadcasted_iota(i32, (ROWS, ROWS), 0)
    q = lax.broadcasted_iota(i32, (ROWS, ROWS), 1)
    before = jnp.where(r < q, 1.0, 0.0).astype(bf16)
    rank = dot(onehot.astype(bf16), before)
    slot = jnp.sum(onehot * (rank + CAP * experts.astype(f32) + 1.0), axis=0, keepdims=True) - 1.0
    return slot.astype(i32)


def slots_col(route_col):
    experts = lax.broadcasted_iota(i32, (ROWS, EXPERTS), 1)
    onehot = jnp.where(experts == route_col, 1.0, 0.0)
    r = lax.broadcasted_iota(i32, (ROWS, ROWS), 0)
    q = lax.broadcasted_iota(i32, (ROWS, ROWS), 1)
    before = jnp.where(q < r, 1.0, 0.0).astype(bf16)
    rank = dot(before, onehot.astype(bf16))
    slot = jnp.sum(onehot * (rank + CAP * experts.astype(f32)), axis=1, keepdims=True)
    return slot.astype(i32)


def kernel(
    live_ref, pos_ref, grow_ref, frow_ref, fcol_ref, gate_ref, hid_ref, og_ref, w_ref, m_ref, fh_ref,
    pw_ref, pm_ref, fo_ref,
    gsend, grecv, gpart, fsend, frecv, rsend, rrecv,
    mnew, wnew, wpart, xm, xw, ym, yw, grad, ortho, gram, poly,
    ssem, rsem, lsem,
):
    idx = lax.axis_index("expert")
    chip, c = idx // 2, idx % 2
    y, z = chip // Z, chip % Z
    partner = {"expert": 2 * chip + 1 - c}

    def peer(u):
        dy, k = u % Y, u // Y
        dz = jnp.where(k % 2 == 1, (k + 1) // 2, Z - k // 2)
        return ((y + dy) % Y) * Z + (z + dz) % Z

    def spread(src_of, dst_ref, n):
        pltpu.make_async_copy(src_of(chip), dst_ref, rsem.at[n]).start()

        @pl.loop(1, CHIPS)
        def _(u):
            t = peer(u)
            pltpu.make_async_remote_copy(
                src_of(t), dst_ref, ssem.at[n], rsem.at[n], device_id={"expert": 2 * t + c}
            ).start()

    def arrived(ref, n):
        pltpu.make_async_copy(ref, ref, rsem.at[n]).wait()

    def to_partner(src_ref, dst_ref, n):
        copy = pltpu.make_async_remote_copy(src_ref, dst_ref, ssem.at[n], rsem.at[n], device_id=partner)
        copy.start()
        return copy

    barrier = pltpu.get_barrier_semaphore()

    @pl.loop(1, CHIPS)
    def _(u):
        pl.semaphore_signal(barrier, inc=1, device_id={"expert": 2 * peer(u) + c})

    pl.semaphore_signal(barrier, inc=1, device_id=partner)

    slot = slots_row(grow_ref[...], live_ref[0])
    slot_ids = lax.broadcasted_iota(i32, (EXPERTS * CAP, ROWS), 0)
    pick = jnp.where(slot_ids == slot, 1.0, 0.0).astype(bf16)
    gsend[:, :, :FF] = dot(pick, hid_ref[...]).reshape(CHIPS, 2 * CAP, FF).astype(bf16)

    @pl.loop(0, D // 256)
    def _(j):
        cols = pl.ds(pl.multiple_of(j * 256, 256), 256)
        out = pl.ds(pl.multiple_of(FF + j * 256, 128), 256)
        gsend[:, :, out] = dot(pick, og_ref[:, cols]).reshape(CHIPS, 2 * CAP, 256).astype(bf16)

    pl.semaphore_wait(barrier, CHIPS)
    spread(lambda t: gsend.at[t], grecv.at[chip], 0)

    fslot = slots_row(frow_ref[...], None)
    fpick = jnp.where(slot_ids == fslot, 1.0, 0.0).astype(bf16)
    fsend[...] = dot(fpick, fh_ref[...]).reshape(CHIPS, 2 * CAP, FF).astype(bf16)
    spread(lambda t: fsend.at[t], frecv.at[chip], 1)

    mine = (lax.broadcasted_iota(i32, (CHIPS, 2 * CAP, 1), 1) // CAP) == c

    def masked_hidden(ref):
        h = ref[:, :, :FF].astype(f32)
        return jnp.where(mine, h, 0.0).reshape(CHIPS * 2 * CAP, FF).astype(bf16)

    def wide_out(ref, cols):
        return ref[:, :, cols].astype(f32).reshape(CHIPS * 2 * CAP, 256).astype(bf16)

    arrived(grecv, 0)
    gcopy = to_partner(grecv, gpart, 2)
    h = masked_hidden(grecv).T

    @pl.loop(0, D // 256)
    def _(j):
        cols = pl.ds(pl.multiple_of(j * 256, 256), 256)
        grad[:, cols] = moment_decay * m_ref[:, cols].astype(f32) + dot(
            h, wide_out(grecv, pl.ds(pl.multiple_of(FF + j * 256, 128), 256))
        )

    gcopy.wait_recv()
    h = masked_hidden(gpart).T

    @pl.loop(0, D // 256)
    def _(j):
        cols = pl.ds(pl.multiple_of(j * 256, 256), 256)
        g = grad[:, cols] + dot(h, wide_out(gpart, pl.ds(pl.multiple_of(FF + j * 256, 128), 256)))
        mnew[:, cols] = g.astype(bf16)

    spread(lambda t: piece(mnew, t), xm.at[c * CHIPS + chip], 3)

    moment = mnew[...].astype(f32)
    frobenius = jnp.sqrt(jnp.sum(moment * moment, keepdims=True))
    ortho[...] = (mnew[...].astype(f32) / (frobenius + norm_floor)).astype(bf16)

    @pl.loop(0, 2)
    def _(_sweep):
        gram[...] = dot(ortho[...], ortho[...], (((1,), (1,)), ((), ()))).astype(bf16)
        squared = dot(gram[...], gram[...])
        poly[...] = (cubic_term * gram[...].astype(f32) + quintic_term * squared).astype(bf16)

        @pl.loop(0, D // 256)
        def _(j):
            cols = pl.ds(pl.multiple_of(j * 256, 256), 256)
            x = ortho[:, cols]
            ortho[:, cols] = (linear_term * x.astype(f32) + dot(poly[...], x)).astype(bf16)

    wnew[...] = (w_ref[...].astype(f32) - step_scale * ortho[...].astype(f32)).astype(bf16)
    wcopy = to_partner(wnew, wpart, 4)
    spread(lambda t: piece(wnew, t), xw.at[c * CHIPS + chip], 5)

    arrived(frecv, 1)
    wcopy.wait_recv()
    x = frecv[...].astype(f32).reshape(CHIPS * 2 * CAP, FF).astype(bf16)

    @pl.loop(0, D // 256)
    def _(j):
        cols = pl.ds(pl.multiple_of(j * 256, 256), 256)
        own = dot(x, wnew[:, cols]).reshape(CHIPS, 2 * CAP, 256)
        other = dot(x, wpart[:, cols]).reshape(CHIPS, 2 * CAP, 256)
        rsend[:, :, cols] = jnp.where(mine, own, other).astype(bf16)

    spread(lambda t: rsend.at[t], rrecv.at[chip], 6)

    def second_hop(x_ref, y_ref, out_ref, first, n):
        own = pl.ds(c * CHIPS, CHIPS)
        arrived(x_ref.at[own], first)
        copy = to_partner(x_ref.at[own], x_ref.at[own], n)
        copy.wait_recv()

        @pl.loop(0, CHIPS)
        def _(t):
            y_ref[t] = x_ref[pos_ref[2 * t + c]]

        spread(lambda t: y_ref.at[t], piece(out_ref, chip), n + 1)
        return copy

    mcopy = second_hop(xm, ym, pm_ref, 3, 7)
    xcopy = second_hop(xw, yw, pw_ref, 5, 9)

    arrived(rrecv, 6)
    fcol = slots_col(fcol_ref[...])
    unpick = jnp.where(lax.broadcasted_iota(i32, (ROWS, EXPERTS * CAP), 1) == fcol, 1.0, 0.0).astype(bf16)

    @pl.loop(0, D // 256)
    def _(j):
        cols = pl.ds(pl.multiple_of(j * 256, 256), 256)
        back = rrecv[:, :, cols].astype(f32).reshape(CHIPS * 2 * CAP, 256).astype(bf16)
        fo_ref[:, cols] = (dot(unpick, back) * gate_ref[...]).astype(bf16)

    arrived(pm_ref, 8)
    arrived(pw_ref, 10)

    for copy in (gcopy, wcopy, mcopy, xcopy):
        copy.wait_send()
    rest = pl.ds(0, CHIPS - 1)
    for ref, n in ((gsend, 0), (fsend, 1), (ym, 3), (yw, 5), (rsend, 6), (ym, 8), (yw, 10)):
        pltpu.make_async_copy(ref.at[rest], ref.at[rest], ssem.at[n]).wait()


def per_device(
    grad_hidden, grad_out, grad_route, live_rows, w_down, w_moment, perm, fwd_hidden, fwd_route, fwd_gate
):
    devices = jnp.arange(EXPERTS, dtype=i32)
    inverse = jnp.sum(jnp.where(perm[None, :] == devices[:, None], devices[None, :], 0), axis=1)
    position = (inverse % 2) * CHIPS + inverse // 2
    smem, vmem = pl.BlockSpec(memory_space=pltpu.SMEM), pl.BlockSpec(memory_space=pltpu.VMEM)
    block = (CHIPS, 2 * CAP)
    pw, pm, fo = pl.pallas_call(
        kernel,
        out_shape=(
            jax.ShapeDtypeStruct((FF, D), bf16),
            jax.ShapeDtypeStruct((FF, D), bf16),
            jax.ShapeDtypeStruct((ROWS, D), bf16),
        ),
        in_specs=[smem, smem] + [vmem] * 9,
        out_specs=(vmem, vmem, vmem),
        scratch_shapes=[
            pltpu.VMEM(block + (WIDE,), bf16),
            pltpu.VMEM(block + (WIDE,), bf16),
            pltpu.VMEM(block + (WIDE,), bf16),
            pltpu.VMEM(block + (FF,), bf16),
            pltpu.VMEM(block + (FF,), bf16),
            pltpu.VMEM(block + (D,), bf16),
            pltpu.VMEM(block + (D,), bf16),
            pltpu.VMEM((FF, D), bf16),
            pltpu.VMEM((FF, D), bf16),
            pltpu.VMEM((FF, D), bf16),
            pltpu.VMEM((EXPERTS, PR, PC), bf16),
            pltpu.VMEM((EXPERTS, PR, PC), bf16),
            pltpu.VMEM((CHIPS, PR, PC), bf16),
            pltpu.VMEM((CHIPS, PR, PC), bf16),
            pltpu.VMEM((FF, D), f32),
            pltpu.VMEM((FF, D), bf16),
            pltpu.VMEM((FF, FF), bf16),
            pltpu.VMEM((FF, FF), bf16),
            pltpu.SemaphoreType.DMA((11,)),
            pltpu.SemaphoreType.DMA((11,)),
            pltpu.SemaphoreType.DMA,
        ],
        compiler_params=pltpu.CompilerParams(collective_id=0, has_side_effects=True),
        name="update_and_move",
    )(
        live_rows, position, grad_route.reshape(1, ROWS), fwd_route.reshape(1, ROWS), fwd_route,
        fwd_gate.reshape(ROWS, 1), grad_hidden, grad_out, w_down[0], w_moment[0], fwd_hidden,
    )
    return pw[None], pm[None], fo


def solution(mesh):
    both = ("layer", "expert")
    in_specs = (
        P(both, None), P(both, None), P(both, None), P(both), P(both, None, None), P(both, None, None),
        P("layer"), P(both, None), P(both, None), P(both),
    )
    out_specs = (P(both, None, None), P(both, None, None), P(both, None))
    return jax.shard_map(per_device, mesh=mesh, in_specs=in_specs, out_specs=out_specs, check_vma=False)
```

```python
import jax
import jax.numpy as jnp
from jax import lax
from jax.experimental import pallas as pl
from jax.experimental.pallas import tpu as pltpu
from jax.sharding import PartitionSpec as P

linear_term = 3.4445
cubic_term = -4.775
quintic_term = 2.0315
moment_decay = 0.9
step_scale = 0.25
norm_floor = 1e-07

Y, Z = 4, 16
CHIPS = Y * Z
EXPERTS = 2 * CHIPS
CAP = 4
ROWS, FF, D = 256, 384, 1024
WIDE = FF + D
PR, PC = 48, 128
PCOLS = D // PC

f32, bf16, i32 = jnp.float32, jnp.bfloat16, jnp.int32


def dot(a, b, dims=(((1,), (0,)), ((), ()))):
    return lax.dot_general(a, b, dims, preferred_element_type=f32)


def piece(ref, p):
    return ref.at[
        pl.ds(pl.multiple_of((p // PCOLS) * PR, 16), PR),
        pl.ds(pl.multiple_of((p % PCOLS) * PC, 128), PC),
    ]


def column(row):
    return jnp.broadcast_to(row, (128, row.shape[1])).T[:, :1]


def slots_row(route_row, live):
    experts = lax.broadcasted_iota(i32, (EXPERTS, ROWS), 0)
    hit = experts == route_row
    if live is not None:
        hit = hit & (lax.broadcasted_iota(i32, (EXPERTS, ROWS), 1) < live)
    onehot = jnp.where(hit, 1.0, 0.0)
    r = lax.broadcasted_iota(i32, (ROWS, ROWS), 0)
    q = lax.broadcasted_iota(i32, (ROWS, ROWS), 1)
    before = jnp.where(r < q, 1.0, 0.0).astype(bf16)
    rank = dot(onehot.astype(bf16), before)
    slot = jnp.sum(onehot * (rank + CAP * experts.astype(f32) + 1.0), axis=0, keepdims=True) - 1.0
    return slot.astype(i32)


def kernel(
    live_ref, perm_in, grow_in, frow_in, gate_in, hid_in, og_in, w_in, m_in, fh_in,
    pw_ref, pm_ref, fo_ref,
    perm_ref, grow_ref, frow_ref, gate_ref, hid_ref, og_ref, w_ref, m_ref, fh_ref, pos_row, pos_ref, unpick, gate_col,
    gsend, grecv, gpart, fsend, frecv, rsend, rrecv,
    mnew, wnew, wpart, xm, xw, ym, yw, grad, ortho, gram, poly,
    ssem, rsem, lsem,
):
    idx = lax.axis_index("expert")
    chip, c = idx // 2, idx % 2
    y, z = chip // Z, chip % Z
    partner = {"expert": 2 * chip + 1 - c}

    def peer(u):
        dy, k = u % Y, u // Y
        dz = jnp.where(k % 2 == 1, (k + 1) // 2, Z - k // 2)
        return ((y + dy) % Y) * Z + (z + dz) % Z

    def spread(src_of, dst_ref, n):
        pltpu.make_async_copy(src_of(chip), dst_ref, rsem.at[n]).start()

        @pl.loop(1, CHIPS)
        def _(u):
            t = peer(u)
            pltpu.make_async_remote_copy(
                src_of(t), dst_ref, ssem.at[n], rsem.at[n], device_id={"expert": 2 * t + c}
            ).start()

    def arrived(ref, n):
        pltpu.make_async_copy(ref, ref, rsem.at[n]).wait()

    def to_partner(src_ref, dst_ref, n):
        copy = pltpu.make_async_remote_copy(src_ref, dst_ref, ssem.at[n], rsem.at[n], device_id=partner)
        copy.start()
        return copy

    barrier = pltpu.get_barrier_semaphore()
    bases = [2 * ((y + dy) % Y) * Z + c for dy in (2, 1, 3, 0)]
    for dz in sorted(range(Z), key=lambda d: -min(d, Z - d)):
        z2 = 2 * ((z + dz) % Z)
        for base in bases[: Y if dz else Y - 1]:
            pl.semaphore_signal(barrier, inc=1, device_id={"expert": base + z2})
    pl.semaphore_signal(barrier, inc=1, device_id=partner)

    loads = [
        pltpu.make_async_copy(src, dst, lsem.at[n])
        for n, (src, dst) in enumerate(
            (
                (grow_in, grow_ref), (hid_in, hid_ref), (og_in, og_ref), (frow_in, frow_ref), (fh_in, fh_ref),
                (gate_in, gate_ref), (perm_in, perm_ref), (m_in, m_ref), (w_in, w_ref),
            )
        )
    ]
    for load in loads:
        load.start()

    loads[0].wait()
    slot = slots_row(grow_ref[...], live_ref[...])
    slot_ids = lax.broadcasted_iota(i32, (EXPERTS * CAP, ROWS), 0)
    pick = jnp.where(slot_ids == slot, 1.0, 0.0).astype(bf16)
    loads[1].wait()
    loads[2].wait()
    gsend[:, :, :FF] = dot(pick, hid_ref[...]).reshape(CHIPS, 2 * CAP, FF).astype(bf16)

    @pl.loop(0, D // 256)
    def _(j):
        cols = pl.ds(pl.multiple_of(j * 256, 256), 256)
        out = pl.ds(pl.multiple_of(FF + j * 256, 128), 256)
        gsend[:, :, out] = dot(pick, og_ref[:, cols]).reshape(CHIPS, 2 * CAP, 256).astype(bf16)

    loads[3].wait()
    fslot = slots_row(frow_ref[...], None)
    fpick = jnp.where(slot_ids == fslot, 1.0, 0.0).astype(bf16)
    loads[4].wait()
    fsend[...] = dot(fpick, fh_ref[...]).reshape(CHIPS, 2 * CAP, FF).astype(bf16)

    pl.semaphore_wait(barrier, CHIPS)
    spread(lambda t: gsend.at[t], grecv.at[chip], 0)
    spread(lambda t: fsend.at[t], frecv.at[chip], 1)

    unpick[...] = fpick.T
    for load in loads[5:]:
        load.wait()
    gate_col[...] = column(gate_ref[...])
    lanes = lax.broadcasted_iota(i32, (EXPERTS, EXPERTS), 1).astype(f32)
    source = lax.broadcasted_iota(i32, (EXPERTS, EXPERTS), 0)
    source = (source % 2) * CHIPS + source // 2
    moves = lanes == column(perm_ref[...].astype(f32))
    pos_row[...] = jnp.max(jnp.where(moves, source, 0), axis=0, keepdims=True)
    pos_copy = pltpu.make_async_copy(pos_row, pos_ref, lsem.at[9])
    pos_copy.start()
    pos_copy.wait()

    mine = (lax.broadcasted_iota(i32, (CHIPS, 2 * CAP, 1), 1) // CAP) == c

    def masked_hidden(ref):
        h = ref[:, :, :FF].astype(f32)
        return jnp.where(mine, h, 0.0).reshape(CHIPS * 2 * CAP, FF).astype(bf16)

    def wide_out(ref, cols):
        return ref[:, :, cols].astype(f32).reshape(CHIPS * 2 * CAP, 256).astype(bf16)

    arrived(grecv, 0)
    gcopy = to_partner(grecv, gpart, 2)
    h = masked_hidden(grecv).T

    @pl.loop(0, D // 256)
    def _(j):
        cols = pl.ds(pl.multiple_of(j * 256, 256), 256)
        grad[:, cols] = moment_decay * m_ref[:, cols].astype(f32) + dot(
            h, wide_out(grecv, pl.ds(pl.multiple_of(FF + j * 256, 128), 256))
        )

    gcopy.wait_recv()
    h = masked_hidden(gpart).T

    @pl.loop(0, D // 256)
    def _(j):
        cols = pl.ds(pl.multiple_of(j * 256, 256), 256)
        g = grad[:, cols] + dot(h, wide_out(gpart, pl.ds(pl.multiple_of(FF + j * 256, 128), 256)))
        mnew[:, cols] = g.astype(bf16)

    spread(lambda t: piece(mnew, t), xm.at[c * CHIPS + chip], 3)

    moment = mnew[...].astype(f32)
    frobenius = jnp.sqrt(jnp.sum(moment * moment, keepdims=True))
    ortho[...] = (mnew[...].astype(f32) / (frobenius + norm_floor)).astype(bf16)

    @pl.loop(0, 2)
    def _(_sweep):
        gram[...] = dot(ortho[...], ortho[...], (((1,), (1,)), ((), ()))).astype(bf16)
        squared = dot(gram[...], gram[...])
        poly[...] = (cubic_term * gram[...].astype(f32) + quintic_term * squared).astype(bf16)

        @pl.loop(0, D // 256)
        def _(j):
            cols = pl.ds(pl.multiple_of(j * 256, 256), 256)
            x = ortho[:, cols]
            ortho[:, cols] = (linear_term * x.astype(f32) + dot(poly[...], x)).astype(bf16)

    wnew[...] = (w_ref[...].astype(f32) - step_scale * ortho[...].astype(f32)).astype(bf16)
    wcopy = to_partner(wnew, wpart, 4)
    spread(lambda t: piece(wnew, t), xw.at[c * CHIPS + chip], 5)

    arrived(frecv, 1)
    wcopy.wait_recv()
    x = frecv[...].astype(f32).reshape(CHIPS * 2 * CAP, FF).astype(bf16)

    @pl.loop(0, D // 256)
    def _(j):
        cols = pl.ds(pl.multiple_of(j * 256, 256), 256)
        own = dot(x, wnew[:, cols]).reshape(CHIPS, 2 * CAP, 256)
        other = dot(x, wpart[:, cols]).reshape(CHIPS, 2 * CAP, 256)
        rsend[:, :, cols] = jnp.where(mine, own, other).astype(bf16)

    spread(lambda t: rsend.at[t], rrecv.at[chip], 6)

    def second_hop(x_ref, y_ref, out_ref, first, n):
        own = pl.ds(c * CHIPS, CHIPS)
        arrived(x_ref.at[own], first)
        copy = to_partner(x_ref.at[own], x_ref.at[own], n)
        copy.wait_recv()

        @pl.loop(0, CHIPS)
        def _(t):
            y_ref[t] = x_ref[pos_ref[0, 2 * t + c]]

        spread(lambda t: y_ref.at[t], piece(out_ref, chip), n + 1)
        return copy

    mcopy = second_hop(xm, ym, pm_ref, 3, 7)
    xcopy = second_hop(xw, yw, pw_ref, 5, 9)

    arrived(rrecv, 6)

    @pl.loop(0, D // 256)
    def _(j):
        cols = pl.ds(pl.multiple_of(j * 256, 256), 256)
        back = rrecv[:, :, cols].astype(f32).reshape(CHIPS * 2 * CAP, 256).astype(bf16)
        fo_ref[:, cols] = (dot(unpick[...], back) * gate_col[...]).astype(bf16)

    arrived(pm_ref, 8)
    arrived(pw_ref, 10)

    for copy in (gcopy, wcopy, mcopy, xcopy):
        copy.wait_send()
    rest = pl.ds(0, CHIPS - 1)
    for ref, n in ((gsend, 0), (fsend, 1), (ym, 3), (yw, 5), (rsend, 6), (ym, 8), (yw, 10)):
        pltpu.make_async_copy(ref.at[rest], ref.at[rest], ssem.at[n]).wait()


def per_device(
    grad_hidden, grad_out, grad_route, live_rows, w_down, w_moment, perm, fwd_hidden, fwd_route, fwd_gate
):
    vmem, hbm = pl.BlockSpec(memory_space=pltpu.VMEM), pl.BlockSpec(memory_space=pltpu.HBM)
    block = (CHIPS, 2 * CAP)
    pw, pm, fo = pl.pallas_call(
        kernel,
        out_shape=(
            pltpu.VMEM((FF, D), bf16),
            pltpu.VMEM((FF, D), bf16),
            pltpu.VMEM((ROWS, D), bf16),
        ),
        in_specs=[vmem] + [hbm] * 9,
        out_specs=(vmem, vmem, vmem),
        scratch_shapes=[
            pltpu.VMEM((1, EXPERTS), i32),
            pltpu.VMEM((1, ROWS), i32),
            pltpu.VMEM((1, ROWS), i32),
            pltpu.VMEM((1, ROWS), f32),
            pltpu.VMEM((ROWS, FF), bf16),
            pltpu.VMEM((ROWS, D), bf16),
            pltpu.VMEM((FF, D), bf16),
            pltpu.VMEM((FF, D), bf16),
            pltpu.VMEM((ROWS, FF), bf16),
            pltpu.VMEM((1, EXPERTS), i32),
            pltpu.SMEM((1, EXPERTS), i32),
            pltpu.VMEM((ROWS, EXPERTS * CAP), bf16),
            pltpu.VMEM((ROWS, 1), f32),
            pltpu.VMEM(block + (WIDE,), bf16),
            pltpu.VMEM(block + (WIDE,), bf16),
            pltpu.VMEM(block + (WIDE,), bf16),
            pltpu.VMEM(block + (FF,), bf16),
            pltpu.VMEM(block + (FF,), bf16),
            pltpu.VMEM(block + (D,), bf16),
            pltpu.VMEM(block + (D,), bf16),
            pltpu.VMEM((FF, D), bf16),
            pltpu.VMEM((FF, D), bf16),
            pltpu.VMEM((FF, D), bf16),
            pltpu.VMEM((EXPERTS, PR, PC), bf16),
            pltpu.VMEM((EXPERTS, PR, PC), bf16),
            pltpu.VMEM((CHIPS, PR, PC), bf16),
            pltpu.VMEM((CHIPS, PR, PC), bf16),
            pltpu.VMEM((FF, D), f32),
            pltpu.VMEM((FF, D), bf16),
            pltpu.VMEM((FF, FF), bf16),
            pltpu.VMEM((FF, FF), bf16),
            pltpu.SemaphoreType.DMA((11,)),
            pltpu.SemaphoreType.DMA((11,)),
            pltpu.SemaphoreType.DMA((10,)),
        ],
        compiler_params=pltpu.CompilerParams(collective_id=0, has_side_effects=True, vmem_limit_bytes=64_930_000),
        name="update_and_move",
    )(
        live_rows.reshape(1, 1), perm.reshape(1, EXPERTS), grad_route.reshape(1, ROWS),
        fwd_route.reshape(1, ROWS), fwd_gate.reshape(1, ROWS),
        grad_hidden, grad_out, w_down[0], w_moment[0], fwd_hidden,
    )
    return pw[None], pm[None], fo


def solution(mesh):
    both = ("layer", "expert")
    in_specs = (
        P(both, None), P(both, None), P(both, None), P(both), P(both, None, None), P(both, None, None),
        P("layer"), P(both, None), P(both, None), P(both),
    )
    out_specs = (P(both, None, None), P(both, None, None), P(both, None))
    return jax.shard_map(per_device, mesh=mesh, in_specs=in_specs, out_specs=out_specs, check_vma=False)
```

```python
import jax
import jax.numpy as jnp
from jax import lax
from jax.experimental import pallas as pl
from jax.experimental.pallas import tpu as pltpu
from jax.sharding import PartitionSpec as P

linear_term = 3.4445
cubic_term = -4.775
quintic_term = 2.0315
moment_decay = 0.9
step_scale = 0.25
norm_floor = 1e-07

Y, Z = 4, 16
CHIPS = Y * Z
EXPERTS = 2 * CHIPS
CAP = 4
ROWS, FF, D = 256, 384, 1024
WIDE = FF + D
PR, PC = 48, 128
PCOLS = D // PC

f32, bf16, i32 = jnp.float32, jnp.bfloat16, jnp.int32


def dot(a, b, dims=(((1,), (0,)), ((), ()))):
    return lax.dot_general(a, b, dims, preferred_element_type=f32)


def piece(ref, p):
    return ref.at[
        pl.ds(pl.multiple_of((p // PCOLS) * PR, 16), PR),
        pl.ds(pl.multiple_of((p % PCOLS) * PC, 128), PC),
    ]


def column(row):
    return jnp.broadcast_to(row, (128, row.shape[1])).T[:, :1]


def slots_row(route_row, live):
    experts = lax.broadcasted_iota(i32, (EXPERTS, ROWS), 0)
    hit = experts == route_row
    if live is not None:
        hit = hit & (lax.broadcasted_iota(i32, (EXPERTS, ROWS), 1) < live)
    onehot = jnp.where(hit, 1.0, 0.0)
    r = lax.broadcasted_iota(i32, (ROWS, ROWS), 0)
    q = lax.broadcasted_iota(i32, (ROWS, ROWS), 1)
    before = jnp.where(r < q, 1.0, 0.0).astype(bf16)
    rank = dot(onehot.astype(bf16), before)
    slot = jnp.sum(onehot * (rank + CAP * experts.astype(f32) + 1.0), axis=0, keepdims=True) - 1.0
    return slot.astype(i32)


def kernel(
    live_ref, perm_in, grow_in, frow_in, gate_in, hid_in, og_in, w_in, m_in, fh_in,
    pw_ref, pm_ref, fo_ref,
    perm_ref, grow_ref, frow_ref, gate_ref, hid_ref, og_ref, w_ref, m_ref, fh_ref, pos_row, pos_ref, unpick, gate_col,
    gsend, grecv, gpart, fsend, frecv, rsend, rrecv,
    mnew, wnew, wpart, xm, xw, ym, yw, grad, ortho, gram, poly,
    ssem, rsem, lsem,
):
    idx = lax.axis_index("expert")
    chip, c = idx // 2, idx % 2
    y, z = chip // Z, chip % Z
    partner = {"expert": 2 * chip + 1 - c}

    def peer(u):
        dy, k = u % Y, u // Y
        dz = jnp.where(k % 2 == 1, (k + 1) // 2, Z - k // 2)
        return ((y + dy) % Y) * Z + (z + dz) % Z

    def spread(src_of, dst_ref, n):
        pltpu.make_async_copy(src_of(chip), dst_ref, rsem.at[n]).start()

        @pl.loop(1, CHIPS)
        def _(u):
            t = peer(u)
            pltpu.make_async_remote_copy(
                src_of(t), dst_ref, ssem.at[n], rsem.at[n], device_id={"expert": 2 * t + c}
            ).start()

    def arrived(ref, n):
        pltpu.make_async_copy(ref, ref, rsem.at[n]).wait()

    def to_partner(src_ref, dst_ref, n):
        copy = pltpu.make_async_remote_copy(src_ref, dst_ref, ssem.at[n], rsem.at[n], device_id=partner)
        copy.start()
        return copy

    barrier = pltpu.get_barrier_semaphore()
    bases = [2 * ((y + dy) % Y) * Z + c for dy in (2, 1, 3, 0)]
    for dz in sorted(range(Z), key=lambda d: -min(d, Z - d)):
        z2 = 2 * ((z + dz) % Z)
        for base in bases[: Y if dz else Y - 1]:
            pl.semaphore_signal(barrier, inc=1, device_id={"expert": base + z2})
    pl.semaphore_signal(barrier, inc=1, device_id=partner)

    loads = [
        pltpu.make_async_copy(src, dst, lsem.at[n])
        for n, (src, dst) in enumerate(
            (
                (grow_in, grow_ref), (hid_in, hid_ref), (og_in, og_ref), (frow_in, frow_ref), (fh_in, fh_ref),
                (gate_in, gate_ref), (perm_in, perm_ref), (m_in, m_ref), (w_in, w_ref),
            )
        )
    ]
    for load in loads:
        load.start()

    loads[0].wait()
    slot = slots_row(grow_ref[...], live_ref[...])
    slot_ids = lax.broadcasted_iota(i32, (EXPERTS * CAP, ROWS), 0)
    pick = jnp.where(slot_ids == slot, 1.0, 0.0).astype(bf16)
    loads[1].wait()
    loads[2].wait()
    gsend[:, :, :FF] = dot(pick, hid_ref[...]).reshape(CHIPS, 2 * CAP, FF).astype(bf16)

    @pl.loop(0, D // 256)
    def _(j):
        cols = pl.ds(pl.multiple_of(j * 256, 256), 256)
        out = pl.ds(pl.multiple_of(FF + j * 256, 128), 256)
        gsend[:, :, out] = dot(pick, og_ref[:, cols]).reshape(CHIPS, 2 * CAP, 256).astype(bf16)

    loads[3].wait()
    fslot = slots_row(frow_ref[...], None)
    fpick = jnp.where(slot_ids == fslot, 1.0, 0.0).astype(bf16)
    loads[4].wait()
    fsend[...] = dot(fpick, fh_ref[...]).reshape(CHIPS, 2 * CAP, FF).astype(bf16)

    pl.semaphore_wait(barrier, CHIPS)
    spread(lambda t: gsend.at[t], grecv.at[chip], 0)
    spread(lambda t: fsend.at[t], frecv.at[chip], 1)

    unpick[...] = fpick.T
    for load in loads[5:]:
        load.wait()
    gate_col[...] = column(gate_ref[...])
    lanes = lax.broadcasted_iota(i32, (EXPERTS, EXPERTS), 1).astype(f32)
    source = lax.broadcasted_iota(i32, (EXPERTS, EXPERTS), 0)
    source = (source % 2) * CHIPS + source // 2
    moves = lanes == column(perm_ref[...].astype(f32))
    pos_row[...] = jnp.max(jnp.where(moves, source, 0), axis=0, keepdims=True)
    pos_copy = pltpu.make_async_copy(pos_row, pos_ref, lsem.at[9])
    pos_copy.start()
    pos_copy.wait()

    mine = (lax.broadcasted_iota(i32, (CHIPS, 2 * CAP, 1), 1) // CAP) == c

    def masked_hidden(ref):
        h = ref[:, :, :FF].astype(f32)
        return jnp.where(mine, h, 0.0).reshape(CHIPS * 2 * CAP, FF).astype(bf16)

    def wide_out(ref, cols):
        return ref[:, :, cols].astype(f32).reshape(CHIPS * 2 * CAP, 256).astype(bf16)

    arrived(grecv, 0)
    gcopy = to_partner(grecv, gpart, 2)
    h = masked_hidden(grecv).T

    @pl.loop(0, D // 256)
    def _(j):
        cols = pl.ds(pl.multiple_of(j * 256, 256), 256)
        grad[:, cols] = moment_decay * m_ref[:, cols].astype(f32) + dot(
            h, wide_out(grecv, pl.ds(pl.multiple_of(FF + j * 256, 128), 256))
        )

    gcopy.wait_recv()
    h = masked_hidden(gpart).T

    @pl.loop(0, D // 256)
    def _(j):
        cols = pl.ds(pl.multiple_of(j * 256, 256), 256)
        g = grad[:, cols] + dot(h, wide_out(gpart, pl.ds(pl.multiple_of(FF + j * 256, 128), 256)))
        mnew[:, cols] = g.astype(bf16)

    spread(lambda t: piece(mnew, t), xm.at[c * CHIPS + chip], 3)

    moment = mnew[...].astype(f32)
    frobenius = jnp.sqrt(jnp.sum(moment * moment, keepdims=True))
    ortho[...] = (mnew[...].astype(f32) / (frobenius + norm_floor)).astype(bf16)

    @pl.loop(0, 2)
    def _(_sweep):
        gram[...] = dot(ortho[...], ortho[...], (((1,), (1,)), ((), ()))).astype(bf16)
        squared = dot(gram[...], gram[...])
        poly[...] = (cubic_term * gram[...].astype(f32) + quintic_term * squared).astype(bf16)

        @pl.loop(0, D // 256)
        def _(j):
            cols = pl.ds(pl.multiple_of(j * 256, 256), 256)
            x = ortho[:, cols]
            ortho[:, cols] = (linear_term * x.astype(f32) + dot(poly[...], x)).astype(bf16)

    wnew[...] = (w_ref[...].astype(f32) - step_scale * ortho[...].astype(f32)).astype(bf16)
    wcopy = to_partner(wnew, wpart, 4)
    spread(lambda t: piece(wnew, t), xw.at[c * CHIPS + chip], 5)

    arrived(frecv, 1)
    wcopy.wait_recv()
    x = frecv[...].astype(f32).reshape(CHIPS * 2 * CAP, FF).astype(bf16)

    @pl.loop(0, D // 256)
    def _(j):
        cols = pl.ds(pl.multiple_of(j * 256, 256), 256)
        own = dot(x, wnew[:, cols]).reshape(CHIPS, 2 * CAP, 256)
        other = dot(x, wpart[:, cols]).reshape(CHIPS, 2 * CAP, 256)
        rsend[:, :, cols] = jnp.where(mine, own, other).astype(bf16)

    spread(lambda t: rsend.at[t], rrecv.at[chip], 6)

    def second_hop(x_ref, y_ref, out_ref, first, n):
        own = pl.ds(c * CHIPS, CHIPS)
        arrived(x_ref.at[own], first)
        copy = to_partner(x_ref.at[own], x_ref.at[own], n)
        copy.wait_recv()

        @pl.loop(0, CHIPS)
        def _(t):
            y_ref[t] = x_ref[pos_ref[0, 2 * t + c]]

        spread(lambda t: y_ref.at[t], piece(out_ref, chip), n + 1)
        return copy

    mcopy = second_hop(xm, ym, pm_ref, 3, 7)
    xcopy = second_hop(xw, yw, pw_ref, 5, 9)

    arrived(rrecv, 6)

    @pl.loop(0, D // 256)
    def _(j):
        cols = pl.ds(pl.multiple_of(j * 256, 256), 256)
        back = rrecv[:, :, cols].astype(f32).reshape(CHIPS * 2 * CAP, 256).astype(bf16)
        fo_ref[:, cols] = (dot(unpick[...], back) * gate_col[...]).astype(bf16)

    arrived(pm_ref, 8)
    arrived(pw_ref, 10)

    for copy in (gcopy, wcopy, mcopy, xcopy):
        copy.wait_send()
    rest = pl.ds(0, CHIPS - 1)
    for ref, n in ((gsend, 0), (fsend, 1), (ym, 3), (yw, 5), (rsend, 6), (ym, 8), (yw, 10)):
        pltpu.make_async_copy(ref.at[rest], ref.at[rest], ssem.at[n]).wait()


def write_out(pw_ref, pm_ref, fo_ref, pw_out, pm_out, fo_out, sem):
    pairs = ((pw_ref, pw_out), (pm_ref, pm_out), (fo_ref, fo_out))
    copies = [pltpu.make_async_copy(src, dst, sem.at[n]) for n, (src, dst) in enumerate(pairs)]
    for copy in copies:
        copy.start()
    for copy in copies:
        copy.wait()


def per_device(
    grad_hidden, grad_out, grad_route, live_rows, w_down, w_moment, perm, fwd_hidden, fwd_route, fwd_gate
):
    vmem, hbm = pl.BlockSpec(memory_space=pltpu.VMEM), pl.BlockSpec(memory_space=pltpu.HBM)
    block = (CHIPS, 2 * CAP)
    pw, pm, fo = pl.pallas_call(
        kernel,
        out_shape=(
            pltpu.VMEM((FF, D), bf16),
            pltpu.VMEM((FF, D), bf16),
            pltpu.VMEM((ROWS, D), bf16),
        ),
        in_specs=[vmem] + [hbm] * 9,
        out_specs=(vmem, vmem, vmem),
        scratch_shapes=[
            pltpu.VMEM((1, EXPERTS), i32),
            pltpu.VMEM((1, ROWS), i32),
            pltpu.VMEM((1, ROWS), i32),
            pltpu.VMEM((1, ROWS), f32),
            pltpu.VMEM((ROWS, FF), bf16),
            pltpu.VMEM((ROWS, D), bf16),
            pltpu.VMEM((FF, D), bf16),
            pltpu.VMEM((FF, D), bf16),
            pltpu.VMEM((ROWS, FF), bf16),
            pltpu.VMEM((1, EXPERTS), i32),
            pltpu.SMEM((1, EXPERTS), i32),
            pltpu.VMEM((ROWS, EXPERTS * CAP), bf16),
            pltpu.VMEM((ROWS, 1), f32),
            pltpu.VMEM(block + (WIDE,), bf16),
            pltpu.VMEM(block + (WIDE,), bf16),
            pltpu.VMEM(block + (WIDE,), bf16),
            pltpu.VMEM(block + (FF,), bf16),
            pltpu.VMEM(block + (FF,), bf16),
            pltpu.VMEM(block + (D,), bf16),
            pltpu.VMEM(block + (D,), bf16),
            pltpu.VMEM((FF, D), bf16),
            pltpu.VMEM((FF, D), bf16),
            pltpu.VMEM((FF, D), bf16),
            pltpu.VMEM((EXPERTS, PR, PC), bf16),
            pltpu.VMEM((EXPERTS, PR, PC), bf16),
            pltpu.VMEM((CHIPS, PR, PC), bf16),
            pltpu.VMEM((CHIPS, PR, PC), bf16),
            pltpu.VMEM((FF, D), f32),
            pltpu.VMEM((FF, D), bf16),
            pltpu.VMEM((FF, FF), bf16),
            pltpu.VMEM((FF, FF), bf16),
            pltpu.SemaphoreType.DMA((11,)),
            pltpu.SemaphoreType.DMA((11,)),
            pltpu.SemaphoreType.DMA((10,)),
        ],
        compiler_params=pltpu.CompilerParams(collective_id=0, has_side_effects=True, vmem_limit_bytes=64_930_000),
        name="update_and_move",
    )(
        live_rows.reshape(1, 1), perm.reshape(1, EXPERTS), grad_route.reshape(1, ROWS),
        fwd_route.reshape(1, ROWS), fwd_gate.reshape(1, ROWS),
        grad_hidden, grad_out, w_down[0], w_moment[0], fwd_hidden,
    )
    pw, pm, fo = pl.pallas_call(
        write_out,
        out_shape=(
            jax.ShapeDtypeStruct((FF, D), bf16),
            jax.ShapeDtypeStruct((FF, D), bf16),
            jax.ShapeDtypeStruct((ROWS, D), bf16),
        ),
        in_specs=[vmem] * 3,
        out_specs=(hbm, hbm, hbm),
        scratch_shapes=[pltpu.SemaphoreType.DMA((3,))],
        compiler_params=pltpu.CompilerParams(vmem_limit_bytes=1 << 20),
        name="write_out",
    )(pw, pm, fo)
    return pw[None], pm[None], fo


def solution(mesh):
    both = ("layer", "expert")
    in_specs = (
        P(both, None), P(both, None), P(both, None), P(both), P(both, None, None), P(both, None, None),
        P("layer"), P(both, None), P(both, None), P(both),
    )
    out_specs = (P(both, None, None), P(both, None, None), P(both, None))
    return jax.shard_map(per_device, mesh=mesh, in_specs=in_specs, out_specs=out_specs, check_vma=False)
```

```python
import jax
import jax.numpy as jnp
from jax import lax
from jax.experimental import pallas as pl
from jax.experimental.pallas import tpu as pltpu
from jax.sharding import PartitionSpec as P

linear_term = 3.4445
cubic_term = -4.775
quintic_term = 2.0315
moment_decay = 0.9
step_scale = 0.25
norm_floor = 1e-07

Y, Z = 4, 16
CHIPS = Y * Z
EXPERTS = 2 * CHIPS
CAP = 4
ROWS, FF, D = 256, 384, 1024
WIDE = FF + D
PR, PC = 48, 128
PCOLS = D // PC

f32, bf16, i32 = jnp.float32, jnp.bfloat16, jnp.int32


def dot(a, b, dims=(((1,), (0,)), ((), ()))):
    return lax.dot_general(a, b, dims, preferred_element_type=f32)


def piece(ref, p):
    return ref.at[
        pl.ds(pl.multiple_of((p // PCOLS) * PR, 16), PR),
        pl.ds(pl.multiple_of((p % PCOLS) * PC, 128), PC),
    ]


def column(row):
    return jnp.broadcast_to(row, (128, row.shape[1])).T[:, :1]


def slots_row(route_row, live):
    experts = lax.broadcasted_iota(i32, (EXPERTS, ROWS), 0)
    hit = experts == route_row
    if live is not None:
        hit = hit & (lax.broadcasted_iota(i32, (EXPERTS, ROWS), 1) < live)
    onehot = jnp.where(hit, 1.0, 0.0)
    r = lax.broadcasted_iota(i32, (ROWS, ROWS), 0)
    q = lax.broadcasted_iota(i32, (ROWS, ROWS), 1)
    before = jnp.where(r < q, 1.0, 0.0).astype(bf16)
    rank = dot(onehot.astype(bf16), before)
    slot = jnp.sum(onehot * (rank + CAP * experts.astype(f32) + 1.0), axis=0, keepdims=True) - 1.0
    return slot.astype(i32)


def kernel(
    live_ref, perm_in, grow_in, frow_in, gate_in, hid_in, og_in, w_in, m_in, fh_in,
    pw_ref, pm_ref, fo_ref,
    perm_ref, grow_ref, frow_ref, gate_ref, hid_ref, og_ref, w_ref, m_ref, fh_ref, pos_row, pos_ref, unpick, gate_col,
    gsend, grecv, gpart, fsend, frecv, rsend, rrecv,
    mnew, wnew, wpart, xm, xw, ym, yw, grad, ortho, gram, poly,
    ssem, rsem, lsem,
):
    idx = lax.axis_index("expert")
    chip, c = idx // 2, idx % 2
    y, z = chip // Z, chip % Z
    partner = {"expert": 2 * chip + 1 - c}

    def peer(u):
        dy, k = (CHIPS - u) % Y, (CHIPS - u) // Y
        dz = jnp.where(k % 2 == 1, (k + 1) // 2, Z - k // 2)
        return ((y + dy) % Y) * Z + (z + dz) % Z

    def spread(src_of, dst_ref, n):
        pltpu.make_async_copy(src_of(chip), dst_ref, rsem.at[n]).start()

        @pl.loop(1, CHIPS)
        def _(u):
            t = peer(u)
            pltpu.make_async_remote_copy(
                src_of(t), dst_ref, ssem.at[n], rsem.at[n], device_id={"expert": 2 * t + c}
            ).start()

    def arrived(ref, n):
        pltpu.make_async_copy(ref, ref, rsem.at[n]).wait()

    def to_partner(src_ref, dst_ref, n):
        copy = pltpu.make_async_remote_copy(src_ref, dst_ref, ssem.at[n], rsem.at[n], device_id=partner)
        copy.start()
        return copy

    barrier = pltpu.get_barrier_semaphore()
    bases = [2 * ((y + dy) % Y) * Z + c for dy in (2, 1, 3, 0)]
    for dz in sorted(range(Z), key=lambda d: -min(d, Z - d)):
        z2 = 2 * ((z + dz) % Z)
        for base in bases[: Y if dz else Y - 1]:
            pl.semaphore_signal(barrier, inc=1, device_id={"expert": base + z2})
    pl.semaphore_signal(barrier, inc=1, device_id=partner)

    loads = [
        pltpu.make_async_copy(src, dst, lsem.at[n])
        for n, (src, dst) in enumerate(
            (
                (grow_in, grow_ref), (hid_in, hid_ref), (og_in, og_ref), (frow_in, frow_ref), (fh_in, fh_ref),
                (gate_in, gate_ref), (perm_in, perm_ref), (m_in, m_ref), (w_in, w_ref),
            )
        )
    ]
    for load in loads:
        load.start()

    loads[0].wait()
    slot = slots_row(grow_ref[...], live_ref[...])
    slot_ids = lax.broadcasted_iota(i32, (EXPERTS * CAP, ROWS), 0)
    pick = jnp.where(slot_ids == slot, 1.0, 0.0).astype(bf16)
    loads[1].wait()
    loads[2].wait()
    gsend[:, :, :FF] = dot(pick, hid_ref[...]).reshape(CHIPS, 2 * CAP, FF).astype(bf16)

    @pl.loop(0, D // 256)
    def _(j):
        cols = pl.ds(pl.multiple_of(j * 256, 256), 256)
        out = pl.ds(pl.multiple_of(FF + j * 256, 128), 256)
        gsend[:, :, out] = dot(pick, og_ref[:, cols]).reshape(CHIPS, 2 * CAP, 256).astype(bf16)

    loads[3].wait()
    fslot = slots_row(frow_ref[...], None)
    fpick = jnp.where(slot_ids == fslot, 1.0, 0.0).astype(bf16)
    loads[4].wait()
    fsend[...] = dot(fpick, fh_ref[...]).reshape(CHIPS, 2 * CAP, FF).astype(bf16)

    pl.semaphore_wait(barrier, CHIPS)
    spread(lambda t: gsend.at[t], grecv.at[chip], 0)
    spread(lambda t: fsend.at[t], frecv.at[chip], 1)

    unpick[...] = fpick.T
    for load in loads[5:]:
        load.wait()
    gate_col[...] = column(gate_ref[...])
    lanes = lax.broadcasted_iota(i32, (EXPERTS, EXPERTS), 1).astype(f32)
    source = lax.broadcasted_iota(i32, (EXPERTS, EXPERTS), 0)
    source = (source % 2) * CHIPS + source // 2
    moves = lanes == column(perm_ref[...].astype(f32))
    pos_row[...] = jnp.max(jnp.where(moves, source, 0), axis=0, keepdims=True)
    pos_copy = pltpu.make_async_copy(pos_row, pos_ref, lsem.at[9])
    pos_copy.start()
    pos_copy.wait()

    mine = (lax.broadcasted_iota(i32, (CHIPS, 2 * CAP, 1), 1) // CAP) == c

    def masked_hidden(ref):
        h = ref[:, :, :FF].astype(f32)
        return jnp.where(mine, h, 0.0).reshape(CHIPS * 2 * CAP, FF).astype(bf16)

    def wide_out(ref, cols):
        return ref[:, :, cols].astype(f32).reshape(CHIPS * 2 * CAP, 256).astype(bf16)

    arrived(grecv, 0)
    gcopy = to_partner(grecv, gpart, 2)
    h = masked_hidden(grecv).T

    @pl.loop(0, D // 256)
    def _(j):
        cols = pl.ds(pl.multiple_of(j * 256, 256), 256)
        grad[:, cols] = moment_decay * m_ref[:, cols].astype(f32) + dot(
            h, wide_out(grecv, pl.ds(pl.multiple_of(FF + j * 256, 128), 256))
        )

    gcopy.wait_recv()
    h = masked_hidden(gpart).T

    @pl.loop(0, D // 256)
    def _(j):
        cols = pl.ds(pl.multiple_of(j * 256, 256), 256)
        g = grad[:, cols] + dot(h, wide_out(gpart, pl.ds(pl.multiple_of(FF + j * 256, 128), 256)))
        mnew[:, cols] = g.astype(bf16)

    spread(lambda t: piece(mnew, t), xm.at[c * CHIPS + chip], 3)

    moment = mnew[...].astype(f32)
    frobenius = jnp.sqrt(jnp.sum(moment * moment, keepdims=True))
    ortho[...] = (mnew[...].astype(f32) / (frobenius + norm_floor)).astype(bf16)

    @pl.loop(0, 2)
    def _(_sweep):
        gram[...] = dot(ortho[...], ortho[...], (((1,), (1,)), ((), ()))).astype(bf16)
        squared = dot(gram[...], gram[...])
        poly[...] = (cubic_term * gram[...].astype(f32) + quintic_term * squared).astype(bf16)

        @pl.loop(0, D // 256)
        def _(j):
            cols = pl.ds(pl.multiple_of(j * 256, 256), 256)
            x = ortho[:, cols]
            ortho[:, cols] = (linear_term * x.astype(f32) + dot(poly[...], x)).astype(bf16)

    wnew[...] = (w_ref[...].astype(f32) - step_scale * ortho[...].astype(f32)).astype(bf16)
    wcopy = to_partner(wnew, wpart, 4)
    spread(lambda t: piece(wnew, t), xw.at[c * CHIPS + chip], 5)

    arrived(frecv, 1)
    wcopy.wait_recv()
    x = frecv[...].astype(f32).reshape(CHIPS * 2 * CAP, FF).astype(bf16)

    @pl.loop(0, D // 256)
    def _(j):
        cols = pl.ds(pl.multiple_of(j * 256, 256), 256)
        own = dot(x, wnew[:, cols]).reshape(CHIPS, 2 * CAP, 256)
        other = dot(x, wpart[:, cols]).reshape(CHIPS, 2 * CAP, 256)
        rsend[:, :, cols] = jnp.where(mine, own, other).astype(bf16)

    spread(lambda t: rsend.at[t], rrecv.at[chip], 6)

    def second_hop(x_ref, y_ref, out_ref, first, n):
        own = pl.ds(c * CHIPS, CHIPS)
        arrived(x_ref.at[own], first)
        copy = to_partner(x_ref.at[own], x_ref.at[own], n)
        copy.wait_recv()

        @pl.loop(0, CHIPS)
        def _(t):
            y_ref[t] = x_ref[pos_ref[0, 2 * t + c]]

        spread(lambda t: y_ref.at[t], piece(out_ref, chip), n + 1)
        return copy

    mcopy = second_hop(xm, ym, pm_ref, 3, 7)
    xcopy = second_hop(xw, yw, pw_ref, 5, 9)

    arrived(rrecv, 6)

    @pl.loop(0, D // 256)
    def _(j):
        cols = pl.ds(pl.multiple_of(j * 256, 256), 256)
        back = rrecv[:, :, cols].astype(f32).reshape(CHIPS * 2 * CAP, 256).astype(bf16)
        fo_ref[:, cols] = (dot(unpick[...], back) * gate_col[...]).astype(bf16)

    arrived(pm_ref, 8)
    arrived(pw_ref, 10)

    for copy in (gcopy, wcopy, mcopy, xcopy):
        copy.wait_send()
    rest = pl.ds(0, CHIPS - 1)
    for ref, n in ((gsend, 0), (fsend, 1), (ym, 3), (yw, 5), (rsend, 6), (ym, 8), (yw, 10)):
        pltpu.make_async_copy(ref.at[rest], ref.at[rest], ssem.at[n]).wait()


def write_out(pw_ref, pm_ref, fo_ref, pw_out, pm_out, fo_out, sem):
    pairs = ((pw_ref, pw_out), (pm_ref, pm_out), (fo_ref, fo_out))
    copies = [pltpu.make_async_copy(src, dst, sem.at[n]) for n, (src, dst) in enumerate(pairs)]
    for copy in copies:
        copy.start()
    for copy in copies:
        copy.wait()


def per_device(
    grad_hidden, grad_out, grad_route, live_rows, w_down, w_moment, perm, fwd_hidden, fwd_route, fwd_gate
):
    vmem, hbm = pl.BlockSpec(memory_space=pltpu.VMEM), pl.BlockSpec(memory_space=pltpu.HBM)
    block = (CHIPS, 2 * CAP)
    pw, pm, fo = pl.pallas_call(
        kernel,
        out_shape=(
            pltpu.VMEM((FF, D), bf16),
            pltpu.VMEM((FF, D), bf16),
            pltpu.VMEM((ROWS, D), bf16),
        ),
        in_specs=[vmem] + [hbm] * 9,
        out_specs=(vmem, vmem, vmem),
        scratch_shapes=[
            pltpu.VMEM((1, EXPERTS), i32),
            pltpu.VMEM((1, ROWS), i32),
            pltpu.VMEM((1, ROWS), i32),
            pltpu.VMEM((1, ROWS), f32),
            pltpu.VMEM((ROWS, FF), bf16),
            pltpu.VMEM((ROWS, D), bf16),
            pltpu.VMEM((FF, D), bf16),
            pltpu.VMEM((FF, D), bf16),
            pltpu.VMEM((ROWS, FF), bf16),
            pltpu.VMEM((1, EXPERTS), i32),
            pltpu.SMEM((1, EXPERTS), i32),
            pltpu.VMEM((ROWS, EXPERTS * CAP), bf16),
            pltpu.VMEM((ROWS, 1), f32),
            pltpu.VMEM(block + (WIDE,), bf16),
            pltpu.VMEM(block + (WIDE,), bf16),
            pltpu.VMEM(block + (WIDE,), bf16),
            pltpu.VMEM(block + (FF,), bf16),
            pltpu.VMEM(block + (FF,), bf16),
            pltpu.VMEM(block + (D,), bf16),
            pltpu.VMEM(block + (D,), bf16),
            pltpu.VMEM((FF, D), bf16),
            pltpu.VMEM((FF, D), bf16),
            pltpu.VMEM((FF, D), bf16),
            pltpu.VMEM((EXPERTS, PR, PC), bf16),
            pltpu.VMEM((EXPERTS, PR, PC), bf16),
            pltpu.VMEM((CHIPS, PR, PC), bf16),
            pltpu.VMEM((CHIPS, PR, PC), bf16),
            pltpu.VMEM((FF, D), f32),
            pltpu.VMEM((FF, D), bf16),
            pltpu.VMEM((FF, FF), bf16),
            pltpu.VMEM((FF, FF), bf16),
            pltpu.SemaphoreType.DMA((11,)),
            pltpu.SemaphoreType.DMA((11,)),
            pltpu.SemaphoreType.DMA((10,)),
        ],
        compiler_params=pltpu.CompilerParams(collective_id=0, has_side_effects=True, vmem_limit_bytes=64_930_000),
        name="update_and_move",
    )(
        live_rows.reshape(1, 1), perm.reshape(1, EXPERTS), grad_route.reshape(1, ROWS),
        fwd_route.reshape(1, ROWS), fwd_gate.reshape(1, ROWS),
        grad_hidden, grad_out, w_down[0], w_moment[0], fwd_hidden,
    )
    pw, pm, fo = pl.pallas_call(
        write_out,
        out_shape=(
            jax.ShapeDtypeStruct((FF, D), bf16),
            jax.ShapeDtypeStruct((FF, D), bf16),
            jax.ShapeDtypeStruct((ROWS, D), bf16),
        ),
        in_specs=[vmem] * 3,
        out_specs=(hbm, hbm, hbm),
        scratch_shapes=[pltpu.SemaphoreType.DMA((3,))],
        compiler_params=pltpu.CompilerParams(vmem_limit_bytes=1 << 20),
        name="write_out",
    )(pw, pm, fo)
    return pw[None], pm[None], fo


def solution(mesh):
    both = ("layer", "expert")
    in_specs = (
        P(both, None), P(both, None), P(both, None), P(both), P(both, None, None), P(both, None, None),
        P("layer"), P(both, None), P(both, None), P(both),
    )
    out_specs = (P(both, None, None), P(both, None, None), P(both, None))
    return jax.shard_map(per_device, mesh=mesh, in_specs=in_specs, out_specs=out_specs, check_vma=False)
```
